1024 devices in a mesh: dp: 32 (over z_lo, core), row: 4 (over x), col: 8 (over y, z_hi).
Axes of the slice: x: 4, y: 4, z: 32 (z_hi: 2, z_lo: 16; z = z_hi * 16 + z_lo), core: 2. Of those that a mesh axis runs over, the one named last changes fastest.
Arguments:
- gate_pre: bfloat16 [4096, 14336], P('dp', 'row'), may hold values from -6 to 6
- up_pre: bfloat16 [4096, 14336], P('dp', 'row'), may hold values from -6 to 6
- down_weight: bfloat16 [14336, 4096], P('row', 'col'), may hold values from -0.046875 to 0.046875
- cotangent: bfloat16 [4096, 4096], P(('dp', 'row'), 'col'), may hold values from -6 to 6
Outputs:
- mixed: bfloat16 [4096, 4096], P(('dp', 'row'), 'col')
- gate_grad: bfloat16 [4096, 14336], P(('dp', 'col'), 'row')
- up_grad: bfloat16 [4096, 14336], P(('dp', 'col'), 'row')
- weight_grad: float32 [14336, 4096], P(('row', 'dp'), 'col')
The draws below stay inside these ranges and needn't reach their ends.
All inputs are finite; a program needn't handle non-finite values.
Results may differ from the reference program's by a relative error of at most 0.017.
Values may be sent and summed in bfloat16 or wider, within the bound.
A program may use at most 64 MiB of HBM per device.

```python
import jax
import jax.numpy as jnp
from jax import lax

D = 4096
FF = 14336
TOK = 128
TOKENS = 4096
N_DP = 32
N_COL = 8


def level_of(stream_key, extent, pieces, smallest, top_value):
    loudness = 1.0
    for position, shards_of in pieces:
        heights = jax.random.uniform(jax.random.fold_in(jax.random.fold_in(stream_key, 6), position), (shards_of,), jnp.float32, smallest / len(pieces), top_value / len(pieces))
        loudness = loudness * jnp.repeat(jnp.exp(heights), extent[position] // shards_of).reshape((-1,) + (1,) * (len(extent) - 1 - position))
    return loudness


def gaussian(rng, shape, spread, bound, pieces=(), held_as=jnp.bfloat16):
    entries = jax.random.normal(rng, shape, jnp.float32) * spread
    if len(pieces) > 0:
        entries = level_of(rng, shape, pieces, -0.22, 0.18) * entries
    return jnp.clip(entries, min=-bound, max=bound).astype(held_as)


def setup_inputs(seed: int = 0) -> dict:
    splits = jax.random.split(jax.random.key(seed), 5)
    gate_pre = gaussian(splits[0], (TOKENS, FF), 1.0, 6.0, ((0, 32), (1, 4)))
    up_pre = gaussian(splits[1], (TOKENS, FF), 1.0, 6.0, ((0, 32), (1, 4)))
    down_weight = gaussian(splits[2], (FF, D), FF ** -0.5, 0.046875, ((0, 4), (1, 8)))
    cotangent = gaussian(splits[3], (TOKENS, D), 1.0, 6.0, ((0, 128), (1, 8)))
    return {"gate_pre": gate_pre, "up_pre": up_pre, "down_weight": down_weight, "cotangent": cotangent}


def reference(gate_pre, up_pre, down_weight, cotangent):
    gate_float = gate_pre.astype(jnp.float32)
    up_float = up_pre.astype(jnp.float32)
    sigmoid_gate = jax.nn.sigmoid(gate_float)
    activated = gate_float * sigmoid_gate
    hidden = (activated * up_float).astype(jnp.bfloat16)
    mixed = jnp.dot(hidden, down_weight, preferred_element_type=jnp.float32).astype(jnp.bfloat16)
    block_width = D // N_COL
    hidden_grad = jnp.zeros((gate_pre.shape[0], FF), jnp.float32)
    for block in range(N_COL):
        cot_block = cotangent[:, block * block_width:(block + 1) * block_width]
        weight_block = down_weight[:, block * block_width:(block + 1) * block_width]
        product = lax.dot_general(cot_block, weight_block, (((1,), (1,)), ((), ())), preferred_element_type=jnp.float32)
        rounded = lax.optimization_barrier(product.astype(jnp.bfloat16))
        hidden_grad = hidden_grad + rounded.astype(jnp.float32)
    gate_grad = (hidden_grad * up_float * sigmoid_gate * (1.0 + gate_float * (1.0 - sigmoid_gate))).astype(jnp.bfloat16)
    up_grad = (hidden_grad * activated).astype(jnp.bfloat16)

    def add_replica(replica, running):
        start = (replica * TOK).astype(jnp.int32)
        hidden_rows = lax.dynamic_slice_in_dim(hidden, start, TOK, 0)
        cot_rows = lax.dynamic_slice_in_dim(cotangent, start, TOK, 0)
        term = lax.dot_general(hidden_rows, cot_rows, (((0,), (0,)), ((), ())), preferred_element_type=jnp.float32)
        return running + term

    weight_sum = lax.fori_loop(jnp.int32(0), jnp.int32(N_DP), add_replica, jnp.zeros((FF, D), jnp.float32))
    weight_grad = weight_sum / jnp.float32(N_DP)
    return mixed, gate_grad, up_grad, weight_grad
```

```python
import functools

import jax
import jax.numpy as jnp
from jax import lax
from jax.experimental import pallas as pl
from jax.experimental.pallas import tpu as pltpu
from jax.sharding import PartitionSpec as P

F32, BF16 = jnp.float32, jnp.bfloat16
ZL, X, Y = 16, 4, 4
TOK, UNITS, COLS = 128, 3584, 512
OWN = TOK // X
HROWS = TOK // (2 * Y)
CH, NCH = 512, UNITS // 512
SHARD = UNITS // ZL
XB = ((0, 1), (1, 1), (2, 2), (4, 4), (8, 4), (12, 4))


def flip(value, mask):
    out = 0
    for bit in (1, 2, 4, 8):
        have = (value // bit) % 2
        out = out + bit * (1 - have if mask & bit else have)
    return out


def kernel(
    gate, up, w, cot, mixed, gate_grad, up_grad, weight_grad,
    hid, hid_t, cg, hg, part, yrecv, ysum, zsend, zrecv, msend, mrecv, acc, arecv,
    cz_s, cz_r, cx_s, cx_r, h_s, h_r, hy_s, hy_r, p_s, p_r, g_s, g_r, m_s, m_r, a_s, a_r,
):
    dp, row, col = lax.axis_index("dp"), lax.axis_index("row"), lax.axis_index("col")
    zl, core = dp // 2, dp % 2
    y, half = col // 2, col % 2
    z = half * ZL + zl
    slot = (zl % 2) * 8 + ((zl // 2) % 2) * 4 + ((zl // 4) % 2) * 2 + zl // 8

    def at_z(to):
        to = (to + 4 * ZL) % (2 * ZL)
        return {"dp": (to % ZL) * 2 + core, "row": row, "col": y * 2 + to // ZL}

    def at_y(to):
        return {"dp": dp, "row": row, "col": ((to + Y) % Y) * 2 + half}

    def at_x(to):
        return {"dp": dp, "row": (to + X) % X, "col": col}

    other_core = {"dp": zl * 2 + 1 - core, "row": row, "col": col}

    def copy(src, dst, send, recv, to):
        return pltpu.make_async_remote_copy(
            src_ref=src, dst_ref=dst, send_sem=send, recv_sem=recv,
            device_id=to, device_id_type=pl.DeviceIdType.MESH,
        )

    barrier = pltpu.get_barrier_semaphore()

    def greet(to):
        pl.semaphore_signal(barrier, inc=1, device_id=to, device_id_type=pl.DeviceIdType.MESH)

    for e in (1, 2, 3):
        greet(at_x(row + e))
        greet(at_y(y + e))
    greet(other_core)

    @pl.loop(0, 8)
    def _(i):
        greet(at_z(z + 1 + i))
        greet(at_z(z - 1 - i))

    greet(at_z(z + ZL))
    pl.semaphore_wait(barrier, 24)

    mine = pl.ds(pl.multiple_of(row * OWN, OWN), OWN)

    def z_block(q, step):
        block = cg.at[flip(slot, q), mine]
        to = at_z(half * ZL + flip(zl, {1: 8, 2: 4, 4: 2, 8: 1}[step]))
        return copy(block, block, cz_s.at[q + step], cz_r.at[q + step], to)

    def z_arrival(q):
        block = cg.at[flip(slot, q), mine]
        return copy(block, block, cz_s.at[q], cz_r.at[q], at_z(z + 1))

    def x_batch(b, e, frm=None):
        first, count = XB[b]
        start = (flip(slot, first) // count) * count
        rows = mine if frm is None else pl.ds(pl.multiple_of(((frm + X) % X) * OWN, OWN), OWN)
        block = cg.at[pl.ds(start, count), rows]
        i = b * 3 + e - 1
        return copy(block, block, cx_s.at[i], cx_r.at[i], at_x(row + e))

    def forward(b):
        for e in (1, 2, 3):
            x_batch(b, e).start()

    def x_arrivals(b):
        for e in (1, 2, 3):
            x_batch(b, e, row - e).wait_recv()

    cg[slot, mine] = cot[...]
    for step in (1, 2, 4, 8):
        z_block(0, step).start()
    forward(0)

    @pl.loop(0, NCH)
    def _(c):
        at = pl.ds(pl.multiple_of(c * CH, CH), CH)
        g = gate[:, at].astype(F32)
        h = (g * jax.nn.sigmoid(g)) * up[:, at].astype(F32)
        hid[:, at] = h.astype(BF16)
        hid_t[at, :] = h.T.astype(BF16)

    z_arrival(1).wait_recv()
    for step in (2, 4, 8):
        z_block(1, step).start()
    forward(1)

    is_source = zl % Y == y

    def hidden_to(e):
        to = z + e - ZL * (e // 9)
        rows = pl.ds(pl.multiple_of(((zl + e) % ZL) * SHARD, 32), SHARD)
        return copy(hid_t.at[rows], hg.at[slot], h_s.at[e], h_r.at[zl // Y], at_z(to))

    @pl.when(is_source)
    def _():
        @pl.loop(1, ZL)
        def _(e):
            hidden_to(e).start()

    for q in (2, 3):
        z_arrival(q).wait_recv()
        for step in (4, 8):
            z_block(q, step).start()
    forward(2)

    x_arrivals(0)

    def part_copy(c, e):
        rows = pl.ds(pl.multiple_of(((y + e) % Y) * 2 * HROWS, 2 * HROWS), 2 * HROWS)
        i = c * 3 + e - 1
        return copy(part.at[c, rows], yrecv.at[c, e - 1], p_s.at[i], p_r.at[i], at_y(y + e))

    @pl.loop(0, NCH)
    def _(c):
        at = pl.ds(pl.multiple_of(c * CH, CH), CH)
        part[c] = lax.dot_general(
            cg[slot], w[at, :], (((1,), (1,)), ((), ())), preferred_element_type=F32
        ).astype(BF16)
        for e in (1, 2, 3):
            part_copy(c, e).start()

    for q in (4, 5, 6, 7):
        z_arrival(q).wait_recv()
        z_block(q, 8).start()
    forward(3)

    def grad_copy(c):
        return copy(zsend.at[c], zrecv.at[c], g_s.at[c], g_r.at[c], at_z(z + ZL))

    @pl.loop(0, NCH)
    def _(c):
        own = pl.ds(pl.multiple_of(y * 2 * HROWS, 2 * HROWS), 2 * HROWS)
        total = part[c, own].astype(F32)
        for e in (1, 2, 3):
            part_copy(c, e).wait_recv()
            total = total + yrecv[c, e - 1].astype(F32)
        ysum[c, 0] = total[:HROWS]
        ysum[c, 1] = total[HROWS:]
        zsend[c] = ysum[c, 1 - half].astype(BF16)
        grad_copy(c).start()

    turn = (y % 2) * 2 + y // 2

    @pl.when(is_source)
    def _():
        hg[slot] = hid_t[pl.ds(pl.multiple_of(zl * SHARD, 32), SHARD), :]

    @pl.loop(0, ZL // Y)
    def _(m):
        @pl.when(y + Y * m != zl)
        def _():
            copy(hid_t.at[pl.ds(0, SHARD)], hg.at[turn * 4 + (m % 2) * 2 + m // 2], h_s.at[0], h_r.at[m], at_z(z + 1)).wait_recv()

    def hidden_on(e, frm):
        t = (frm % 2) * 2 + frm // 2
        block = hg.at[pl.ds(t * 4, 4)]
        return copy(block, block, hy_s.at[e - 1], hy_r.at[e - 1], at_y(y + e))

    for e in (1, 2, 3):
        hidden_on(e, y).start()

    for b in (4, 5):
        for q in range(XB[b][0], XB[b][0] + 4):
            z_arrival(q).wait_recv()
        forward(b)

    def mixed_copy(e):
        return copy(msend.at[(row + e) % X], mrecv.at[e - 1], m_s.at[e - 1], m_r.at[e - 1], at_x(row + e))

    partial = jnp.dot(hid[...], w[...], preferred_element_type=F32)
    for r in range(X):
        msend[r] = partial[r * OWN : (r + 1) * OWN].astype(BF16)
    for e in (1, 2, 3):
        mixed_copy(e).start()

    for e in (1, 2, 3):
        hidden_on(e, (y - e + Y) % Y).wait_recv()
    for b in range(1, len(XB)):
        x_arrivals(b)

    acc[...] = jnp.zeros_like(acc)

    @pl.loop(0, ZL)
    def _(p):
        product = jnp.dot(hg[p], cg[p], preferred_element_type=F32)
        acc[0] += product[: SHARD // 2]
        acc[1] += product[SHARD // 2 :]

    swap = copy(acc.at[1 - core], arecv, a_s, a_r, other_core)
    swap.start()

    total = msend[row].astype(F32)
    for e in (1, 2, 3):
        mixed_copy(e).wait_recv()
        total = total + mrecv[e - 1].astype(F32)
    mixed[...] = total.astype(BF16)

    swap.wait_recv()
    weight_grad[...] = (acc[core] + arecv[...]) * (1.0 / (2 * ZL))

    @pl.loop(0, NCH)
    def _(c):
        at = pl.ds(pl.multiple_of(c * CH, CH), CH)
        rows = pl.ds(pl.multiple_of(col * HROWS, HROWS), HROWS)
        g = gate[rows, at].astype(F32)
        u = up[rows, at].astype(F32)
        s = jax.nn.sigmoid(g)
        grad_copy(c).wait_recv()
        hidden_grad = ysum[c, half] + zrecv[c].astype(F32)
        gate_grad[:, at] = (hidden_grad * u * s * (1.0 + g * (1.0 - s))).astype(BF16)
        up_grad[:, at] = (hidden_grad * (g * s)).astype(BF16)

    for step in (1, 2, 4, 8):
        for q in range(step):
            z_block(q, step).wait_send()
    for b in range(len(XB)):
        for e in (1, 2, 3):
            x_batch(b, e).wait_send()

    @pl.when(is_source)
    def _():
        @pl.loop(1, ZL)
        def _(e):
            hidden_to(e).wait_send()

    @pl.loop(0, NCH)
    def _(c):
        for e in (1, 2, 3):
            part_copy(c, e).wait_send()
        grad_copy(c).wait_send()

    for e in (1, 2, 3):
        hidden_on(e, y).wait_send()
        mixed_copy(e).wait_send()
    swap.wait_send()


def body(gate_pre, up_pre, down_weight, cotangent):
    vmem = pl.BlockSpec(memory_space=pltpu.VMEM)
    dma = pltpu.SemaphoreType.DMA
    pair = lambda n: [dma((n,)), dma((n,))]
    return pl.pallas_call(
        kernel,
        name="mlp",
        out_shape=(
            jax.ShapeDtypeStruct((OWN, COLS), BF16),
            jax.ShapeDtypeStruct((HROWS, UNITS), BF16),
            jax.ShapeDtypeStruct((HROWS, UNITS), BF16),
            jax.ShapeDtypeStruct((SHARD // 2, COLS), F32),
        ),
        in_specs=[vmem] * 4,
        out_specs=(vmem,) * 4,
        scratch_shapes=[
            pltpu.VMEM((TOK, UNITS), BF16),
            pltpu.VMEM((UNITS, TOK), BF16),
            pltpu.VMEM((ZL, TOK, COLS), BF16),
            pltpu.VMEM((ZL, SHARD, TOK), BF16),
            pltpu.VMEM((NCH, TOK, CH), BF16),
            pltpu.VMEM((NCH, 3, 2 * HROWS, CH), BF16),
            pltpu.VMEM((NCH, 2, HROWS, CH), F32),
            pltpu.VMEM((NCH, HROWS, CH), BF16),
            pltpu.VMEM((NCH, HROWS, CH), BF16),
            pltpu.VMEM((X, OWN, COLS), BF16),
            pltpu.VMEM((3, OWN, COLS), BF16),
            pltpu.VMEM((2, SHARD // 2, COLS), F32),
            pltpu.VMEM((SHARD // 2, COLS), F32),
            *pair(16), *pair(3 * len(XB)), *pair(16), *pair(3), *pair(3 * NCH), *pair(NCH), *pair(3),
            dma, dma,
        ],
        compiler_params=pltpu.CompilerParams(
            collective_id=0, has_side_effects=True, vmem_limit_bytes=40 << 20
        ),
    )(gate_pre, up_pre, down_weight, cotangent)


def solution(mesh):
    placed = (P("dp", "row"), P("dp", "row"), P("row", "col"), P(("dp", "row"), "col"))
    return jax.shard_map(
        body,
        mesh=mesh,
        in_specs=placed,
        out_specs=(
            P(("dp", "row"), "col"),
            P(("dp", "col"), "row"),
            P(("dp", "col"), "row"),
            P(("row", "dp"), "col"),
        ),
        check_vma=False,
    )
```

```python
import functools

import jax
import jax.numpy as jnp
from jax import lax
from jax.experimental import pallas as pl
from jax.experimental.pallas import tpu as pltpu
from jax.sharding import PartitionSpec as P

F32, BF16 = jnp.float32, jnp.bfloat16
ZL, X, Y = 16, 4, 4
TOK, UNITS, COLS = 128, 3584, 512
OWN = TOK // X
HROWS = TOK // (2 * Y)
CH, NCH = 512, UNITS // 512
SHARD = UNITS // ZL
PIECE, PAD = SHARD // Y, 64
XB = ((0, 1), (1, 1), (2, 2), (4, 4), (8, 4), (12, 4))
HB = ((4, 8), (0, 4), (12, 4))


def flip(value, mask):
    out = 0
    for bit in (1, 2, 4, 8):
        have = (value // bit) % 2
        out = out + bit * (1 - have if mask & bit else have)
    return out


def kernel(
    gate_in, up_in, w_in, cot_in, mixed_out, gate_grad_out, up_grad_out, weight_grad_out,
    mixed, gate_grad, up_grad, weight_grad, gate_factor, up_factor, gate, up, w, hid, hid_t, cg, hsend, hg, part, yrecv, ysum, zsend, zrecv, msend, mrecv, acc, arecv,
    in_s, out_s, cz_s, cz_r, cx_s, cx_r, h_s, h_r, hy_s, hy_r, p_s, p_r, g_s, g_r, m_s, m_r, a_s, a_r,
):
    dp, row, col = lax.axis_index("dp"), lax.axis_index("row"), lax.axis_index("col")
    zl, core = dp // 2, dp % 2
    y, half = col // 2, col % 2
    z = half * ZL + zl

    def bits_reversed(j):
        return (j % 2) * 8 + ((j // 2) % 2) * 4 + ((j // 4) % 2) * 2 + j // 8

    slot = bits_reversed(zl)
    mine = pl.ds(pl.multiple_of(row * OWN, OWN), OWN)
    load_cot = pltpu.make_async_copy(cot_in, cg.at[slot, mine], in_s.at[0])
    load_w = pltpu.make_async_copy(w_in, w, in_s.at[1])
    load_gate = pltpu.make_async_copy(gate_in, gate, in_s.at[2])
    load_up = pltpu.make_async_copy(up_in, up, in_s.at[3])
    for load in (load_cot, load_gate, load_up, load_w):
        load.start()

    def at_z(to):
        to = (to + 4 * ZL) % (2 * ZL)
        return {"dp": (to % ZL) * 2 + core, "row": row, "col": y * 2 + to // ZL}

    def at_y(to):
        return {"dp": dp, "row": row, "col": ((to + Y) % Y) * 2 + half}

    def at_x(to):
        return {"dp": dp, "row": (to + X) % X, "col": col}

    other_core = {"dp": zl * 2 + 1 - core, "row": row, "col": col}

    def copy(src, dst, send, recv, to):
        return pltpu.make_async_remote_copy(
            src_ref=src, dst_ref=dst, send_sem=send, recv_sem=recv,
            device_id=to, device_id_type=pl.DeviceIdType.MESH,
        )

    barrier = pltpu.get_barrier_semaphore()

    def greet(to):
        pl.semaphore_signal(barrier, inc=1, device_id=to, device_id_type=pl.DeviceIdType.MESH)

    for e in (1, 2, 3):
        greet(at_x(row + e))
        greet(at_y(y + e))
    greet(other_core)

    @pl.loop(0, 8)
    def _(i):
        greet(at_z(z + 1 + i))
        greet(at_z(z - 1 - i))

    load_gate.wait()
    load_up.wait()

    @pl.loop(0, NCH)
    def _(c):
        at = pl.ds(pl.multiple_of(c * CH, CH), CH)
        g = gate[:, at].astype(F32)
        h = (g * jax.nn.sigmoid(g)) * up[:, at].astype(F32)
        hid[:, at] = h.astype(BF16)
        hid_t[at, :] = h.T

    def piece(i):
        rows = pl.ds(pl.multiple_of(i * SHARD + y * PIECE, 8), PIECE)
        return jnp.concatenate([hid_t[rows, :], jnp.zeros((PAD - PIECE, TOK), F32)], axis=0).astype(BF16)

    def piece_to(f):
        return copy(hsend.at[f], hg.at[f, y], h_s.at[f], h_r.at[f], at_z(z + f - 8))

    def send_pieces():
        @pl.loop(0, ZL)
        def _(f):
            @pl.when(f != 8)
            def _():
                piece_to(f).start()

    hg[8, y] = piece(zl)

    @pl.loop(0, ZL)
    def _(f):
        @pl.when(f != 8)
        def _():
            hsend[f] = piece((zl + f + 8) % ZL)

    pl.semaphore_wait(barrier, 23)

    def z_block(q, step):
        block = cg.at[flip(slot, q), mine]
        to = at_z(half * ZL + flip(zl, {1: 8, 2: 4, 4: 2, 8: 1}[step]))
        return copy(block, block, cz_s.at[q + step], cz_r.at[q + step], to)

    def z_arrival(q):
        block = cg.at[flip(slot, q), mine]
        return copy(block, block, cz_s.at[q], cz_r.at[q], at_z(z + 1))

    def x_batch(b, e, frm=None):
        first, count = XB[b]
        start = (flip(slot, first) // count) * count
        rows = mine if frm is None else pl.ds(pl.multiple_of(((frm + X) % X) * OWN, OWN), OWN)
        block = cg.at[pl.ds(start, count), rows]
        i = b * 3 + e - 1
        return copy(block, block, cx_s.at[i], cx_r.at[i], at_x(row + e))

    def forward(b):
        for e in (1, 2, 3):
            x_batch(b, e).start()

    def x_arrivals(b):
        for e in (1, 2, 3):
            x_batch(b, e, row - e).wait_recv()

    load_cot.wait()
    forward(0)
    for step in (1, 2, 4, 8):
        z_block(0, step).start()

    send_pieces()

    def part_copy(c, e):
        rows = pl.ds(pl.multiple_of(((y + e) % Y) * 2 * HROWS, 2 * HROWS), 2 * HROWS)
        i = c * 3 + e - 1
        return copy(part.at[c, rows], yrecv.at[c, e - 1], p_s.at[i], p_r.at[i], at_y(y + e))

    def part_chunks(first, last):
        @pl.loop(first, last)
        def _(c):
            at = pl.ds(pl.multiple_of(c * CH, CH), CH)
            part[c] = lax.dot_general(
                cg[slot], w[at, :], (((1,), (1,)), ((), ())), preferred_element_type=F32
            ).astype(BF16)
            for e in (1, 2, 3):
                part_copy(c, e).start()

    load_w.wait()
    x_arrivals(0)
    part_chunks(0, 1)
    z_arrival(1).wait_recv()
    for step in (2, 4, 8):
        z_block(1, step).start()
    forward(1)
    part_chunks(1, 4)
    for q in (2, 3):
        z_arrival(q).wait_recv()
        for step in (4, 8):
            z_block(q, step).start()
    forward(2)
    part_chunks(4, NCH)

    def grad_copy(c):
        return copy(zsend.at[c], zrecv.at[c], g_s.at[c], g_r.at[c], at_z(z + ZL))

    def sum_chunks(first, last):
        @pl.loop(first, last)
        def _(c):
            own = pl.ds(pl.multiple_of(y * 2 * HROWS, 2 * HROWS), 2 * HROWS)
            total = part[c, own].astype(F32)
            for e in (1, 2, 3):
                part_copy(c, e).wait_recv()
                total = total + yrecv[c, e - 1].astype(F32)
            ysum[c, 0] = total[:HROWS]
            ysum[c, 1] = total[HROWS:]
            zsend[c] = ysum[c, 1 - half].astype(BF16)
            grad_copy(c).start()

    sum_chunks(0, 3)
    for q in (4, 5, 6, 7):
        z_arrival(q).wait_recv()
        z_block(q, 8).start()
    forward(3)
    sum_chunks(3, NCH)


    def mixed_copy(e):
        return copy(msend.at[(row + e) % X], mrecv.at[e - 1], m_s.at[e - 1], m_r.at[e - 1], at_x(row + e))

    partial = jnp.dot(hid[...], w[...], preferred_element_type=F32)
    for r in range(X):
        msend[r] = partial[r * OWN : (r + 1) * OWN].astype(BF16)
    for e in (1, 2, 3):
        mixed_copy(e).start()

    @pl.loop(0, NCH)
    def _(c):
        at = pl.ds(pl.multiple_of(c * CH, CH), CH)
        rows = pl.ds(pl.multiple_of(col * HROWS, HROWS), HROWS)
        g = gate[rows, at].astype(F32)
        sg = jax.nn.sigmoid(g)
        gate_factor[c] = up[rows, at].astype(F32) * sg * (1.0 + g * (1.0 - sg))
        up_factor[c] = g * sg

    def piece_on(b, e, frm):
        first, count = HB[b]
        block = hg.at[pl.ds(first, count), frm]
        i = b * 3 + e - 1
        return copy(block, block, hy_s.at[i], hy_r.at[i], at_y(y + e))

    for b, (first, count) in enumerate(HB):
        for f in range(first, first + count):
            if f != 8:
                piece_to(f).wait_recv()
        for e in (1, 2, 3):
            piece_on(b, e, y).start()

    for b in (4, 5):
        for q in range(XB[b][0], XB[b][0] + 4):
            z_arrival(q).wait_recv()
        forward(b)

    for b in range(len(HB)):
        for e in (1, 2, 3):
            piece_on(b, e, (y - e + Y) % Y).wait_recv()
    for b in range(1, len(XB)):
        x_arrivals(b)

    acc[...] = jnp.zeros_like(acc)

    @pl.loop(0, ZL)
    def _(f):
        product = jnp.dot(
            hg[f].reshape(Y * PAD, TOK), cg[bits_reversed((zl + 8 - f + ZL) % ZL)], preferred_element_type=F32
        )
        for q in range(Y):
            acc[q // 2, (q % 2) * PIECE : (q % 2 + 1) * PIECE] += product[q * PAD : q * PAD + PIECE]

    swap = copy(acc.at[1 - core], arecv, a_s, a_r, other_core)
    swap.start()

    total = msend[row].astype(F32)
    for e in (1, 2, 3):
        mixed_copy(e).wait_recv()
        total = total + mrecv[e - 1].astype(F32)
    mixed[...] = total.astype(BF16)
    store_mixed = pltpu.make_async_copy(mixed, mixed_out, out_s.at[0])
    store_mixed.start()

    swap.wait_recv()
    weight_grad[...] = (acc[core] + arecv[...]) * (1.0 / (2 * ZL))
    store_weight = pltpu.make_async_copy(weight_grad, weight_grad_out, out_s.at[1])
    store_weight.start()

    @pl.loop(0, NCH)
    def _(c):
        at = pl.ds(pl.multiple_of(c * CH, CH), CH)
        grad_copy(c).wait_recv()
        hidden_grad = ysum[c, half] + zrecv[c].astype(F32)
        gate_grad[:, at] = (hidden_grad * gate_factor[c]).astype(BF16)
        up_grad[:, at] = (hidden_grad * up_factor[c]).astype(BF16)

    store_gate = pltpu.make_async_copy(gate_grad, gate_grad_out, out_s.at[2])
    store_up = pltpu.make_async_copy(up_grad, up_grad_out, out_s.at[3])
    store_gate.start()
    store_up.start()

    for step in (1, 2, 4, 8):
        for q in range(step):
            z_block(q, step).wait_send()
    for b in range(len(XB)):
        for e in (1, 2, 3):
            x_batch(b, e).wait_send()

    @pl.loop(0, ZL)
    def _(f):
        @pl.when(f != 8)
        def _():
            piece_to(f).wait_send()

    @pl.loop(0, NCH)
    def _(c):
        for e in (1, 2, 3):
            part_copy(c, e).wait_send()
        grad_copy(c).wait_send()

    for e in (1, 2, 3):
        for b in range(len(HB)):
            piece_on(b, e, y).wait_send()
        mixed_copy(e).wait_send()
    swap.wait_send()
    for store in (store_mixed, store_weight, store_gate, store_up):
        store.wait()


def body(gate_pre, up_pre, down_weight, cotangent):
    hbm = pl.BlockSpec(memory_space=pltpu.HBM)
    dma = pltpu.SemaphoreType.DMA
    pair = lambda n: [dma((n,)), dma((n,))]
    return pl.pallas_call(
        kernel,
        name="mlp",
        out_shape=(
            jax.ShapeDtypeStruct((OWN, COLS), BF16),
            jax.ShapeDtypeStruct((HROWS, UNITS), BF16),
            jax.ShapeDtypeStruct((HROWS, UNITS), BF16),
            jax.ShapeDtypeStruct((SHARD // 2, COLS), F32),
        ),
        in_specs=[hbm] * 4,
        out_specs=(hbm,) * 4,
        scratch_shapes=[
            pltpu.VMEM((OWN, COLS), BF16),
            pltpu.VMEM((HROWS, UNITS), BF16),
            pltpu.VMEM((HROWS, UNITS), BF16),
            pltpu.VMEM((SHARD // 2, COLS), F32),
            pltpu.VMEM((NCH, HROWS, CH), F32),
            pltpu.VMEM((NCH, HROWS, CH), F32),
            pltpu.VMEM((TOK, UNITS), BF16),
            pltpu.VMEM((TOK, UNITS), BF16),
            pltpu.VMEM((UNITS, COLS), BF16),
            pltpu.VMEM((TOK, UNITS), BF16),
            pltpu.VMEM((UNITS, TOK), F32),
            pltpu.VMEM((ZL, TOK, COLS), BF16),
            pltpu.VMEM((ZL, PAD, TOK), BF16),
            pltpu.VMEM((ZL, Y, PAD, TOK), BF16),
            pltpu.VMEM((NCH, TOK, CH), BF16),
            pltpu.VMEM((NCH, 3, 2 * HROWS, CH), BF16),
            pltpu.VMEM((NCH, 2, HROWS, CH), F32),
            pltpu.VMEM((NCH, HROWS, CH), BF16),
            pltpu.VMEM((NCH, HROWS, CH), BF16),
            pltpu.VMEM((X, OWN, COLS), BF16),
            pltpu.VMEM((3, OWN, COLS), BF16),
            pltpu.VMEM((2, SHARD // 2, COLS), F32),
            pltpu.VMEM((SHARD // 2, COLS), F32),
            dma((4,)), dma((4,)), *pair(16), *pair(3 * len(XB)), *pair(ZL), *pair(3 * len(HB)), *pair(3 * NCH), *pair(NCH), *pair(3),
            dma, dma,
        ],
        compiler_params=pltpu.CompilerParams(
            collective_id=0, has_side_effects=True, vmem_limit_bytes=60 << 20
        ),
    )(gate_pre, up_pre, down_weight, cotangent)


def solution(mesh):
    placed = (P("dp", "row"), P("dp", "row"), P("row", "col"), P(("dp", "row"), "col"))
    return jax.shard_map(
        body,
        mesh=mesh,
        in_specs=placed,
        out_specs=(
            P(("dp", "row"), "col"),
            P(("dp", "col"), "row"),
            P(("dp", "col"), "row"),
            P(("row", "dp"), "col"),
        ),
        check_vma=False,
    )
```

```python
import functools

import jax
import jax.numpy as jnp
from jax import lax
from jax.experimental import pallas as pl
from jax.experimental.pallas import tpu as pltpu
from jax.sharding import PartitionSpec as P

F32, BF16 = jnp.float32, jnp.bfloat16
ZL, X, Y = 16, 4, 4
TOK, UNITS, COLS = 128, 3584, 512
OWN = TOK // X
HROWS = TOK // (2 * Y)
CH, NCH = 512, UNITS // 512
SHARD = UNITS // ZL
PIECE = 2 * SHARD // Y
NT = ZL // 2
XB = ((0, 1), (1, 1), (2, 2), (4, 2), (6, 2))
HB = ((2, 4), (0, 2), (6, 2))


def flip(value, mask):
    out = 0
    for bit in (1, 2, 4, 8):
        have = (value // bit) % 2
        out = out + bit * (1 - have if mask & bit else have)
    return out


def kernel(
    gate_in, up_in, w_in, cot_in, mixed_out, gate_grad_out, up_grad_out, weight_grad_out,
    mixed, gate_grad, up_grad, weight_grad, gate_factor, up_factor, gate, up, w, hid, hid_t, cg, hg, part, yrecv, ysum, zsend, zrecv, msend, mrecv, acc, arecv, nsend, nrecv,
    in_s, out_s, cz_s, cz_r, cx_s, cx_r, h_s, h_r, hy_s, hy_r, p_s, p_r, g_s, g_r, m_s, m_r, a_s, a_r, n_s, n_r,
):
    dp, row, col = lax.axis_index("dp"), lax.axis_index("row"), lax.axis_index("col")
    zl, core = dp // 2, dp % 2
    y, half = col // 2, col % 2
    z = half * ZL + zl

    def slot_of(j):
        return ((j // 2) % 2) * 4 + ((j // 4) % 2) * 2 + j // 8

    slot = slot_of(zl)
    mine = pl.ds(pl.multiple_of(row * OWN, OWN), OWN)
    load_cot = pltpu.make_async_copy(cot_in, cg.at[slot, mine], in_s.at[0])
    load_w = pltpu.make_async_copy(w_in, w, in_s.at[1])
    load_gate = pltpu.make_async_copy(gate_in, gate, in_s.at[2])
    load_up = pltpu.make_async_copy(up_in, up, in_s.at[3])
    for load in (load_cot, load_gate, load_up, load_w):
        load.start()

    def at_z(to):
        to = (to + 4 * ZL) % (2 * ZL)
        return {"dp": (to % ZL) * 2 + core, "row": row, "col": y * 2 + to // ZL}

    def at_y(to):
        return {"dp": dp, "row": row, "col": ((to + Y) % Y) * 2 + half}

    def at_x(to):
        return {"dp": dp, "row": (to + X) % X, "col": col}

    other_core = {"dp": zl * 2 + 1 - core, "row": row, "col": col}
    odd = zl % 2
    next_zl = flip(zl, 1)
    next_chip = ({"dp": next_zl * 2 + core, "row": row, "col": col}, {"dp": next_zl * 2 + 1 - core, "row": row, "col": col})

    def copy(src, dst, send, recv, to):
        return pltpu.make_async_remote_copy(
            src_ref=src, dst_ref=dst, send_sem=send, recv_sem=recv,
            device_id=to, device_id_type=pl.DeviceIdType.MESH,
        )

    barrier = pltpu.get_barrier_semaphore()

    def greet(to):
        pl.semaphore_signal(barrier, inc=1, device_id=to, device_id_type=pl.DeviceIdType.MESH)

    for e in (1, 2, 3):
        greet(at_x(row + e))
        greet(at_y(y + e))
    greet(other_core)
    greet(next_chip[0])
    greet(next_chip[1])

    @pl.loop(1, 5)
    def _(i):
        greet(at_z(z + 2 * i))
        greet(at_z(z - 2 * i))

    load_gate.wait()
    load_up.wait()

    @pl.loop(0, NCH)
    def _(c):
        at = pl.ds(pl.multiple_of(c * CH, CH), CH)
        g = gate[:, at].astype(F32)
        h = (g * jax.nn.sigmoid(g)) * up[:, at].astype(F32)
        hid[:, at] = h.astype(BF16)
        hid_t[at, :] = h.T.astype(BF16)

    def piece(i):
        return pl.ds(pl.multiple_of((i // 2) * 2 * SHARD + y * PIECE, 16), PIECE)

    def piece_to(g):
        rows = piece((zl + 2 * g + 8) % ZL)
        far = (1 - jnp.minimum(g, 1)) * ((zl // 2) % 2) * ZL
        return copy(hid_t.at[rows], hg.at[g, y], h_s.at[g], h_r.at[g], at_z(z + 2 * g - 8 + far))

    def send_pieces():
        @pl.loop(0, NT)
        def _(g):
            @pl.when(g != 4)
            def _():
                piece_to(g).start()

    hg[4, y] = hid_t[piece(zl), :]
    pl.semaphore_wait(barrier, 17)

    def z_block(q, step):
        block = cg.at[flip(slot, q), mine]
        to = at_z(half * ZL + flip(zl, {1: 8, 2: 4, 4: 2}[step]))
        return copy(block, block, cz_s.at[q + step], cz_r.at[q + step], to)

    def z_arrival(q):
        block = cg.at[flip(slot, q), mine]
        return copy(block, block, cz_s.at[q], cz_r.at[q], at_z(z + 1))

    def x_batch(b, e, frm=None):
        first, count = XB[b]
        start = (flip(slot, first) // count) * count
        rows = mine if frm is None else pl.ds(pl.multiple_of(((frm + X) % X) * OWN, OWN), OWN)
        block = cg.at[pl.ds(start, count), rows]
        i = b * 3 + e - 1
        return copy(block, block, cx_s.at[i], cx_r.at[i], at_x(row + e))

    def forward(b):
        for e in (1, 2, 3):
            x_batch(b, e).start()

    def x_arrivals(b):
        for e in (1, 2, 3):
            x_batch(b, e, row - e).wait_recv()

    load_cot.wait()
    forward(0)
    for step in (1, 2, 4):
        z_block(0, step).start()

    send_pieces()

    def part_copy(c, e):
        rows = pl.ds(pl.multiple_of(((y + e) % Y) * 2 * HROWS, 2 * HROWS), 2 * HROWS)
        i = c * 3 + e - 1
        return copy(part.at[c, rows], yrecv.at[c, e - 1], p_s.at[i], p_r.at[i], at_y(y + e))

    def part_chunks(first, last):
        @pl.loop(first, last)
        def _(c):
            at = pl.ds(pl.multiple_of(c * CH, CH), CH)
            part[c] = lax.dot_general(
                cg[slot], w[at, :], (((1,), (1,)), ((), ())), preferred_element_type=F32
            ).astype(BF16)
            for e in (1, 2, 3):
                part_copy(c, e).start()

    def grad_copy(c):
        return copy(zsend.at[c], zrecv.at[c], g_s.at[c], g_r.at[c], at_z(z + ZL))

    def sum_chunks(first, last):
        @pl.loop(first, last)
        def _(c):
            own = pl.ds(pl.multiple_of(y * 2 * HROWS, 2 * HROWS), 2 * HROWS)
            total = part[c, own].astype(F32)
            for e in (1, 2, 3):
                part_copy(c, e).wait_recv()
                total = total + yrecv[c, e - 1].astype(F32)
            ysum[c, 0] = total[:HROWS]
            ysum[c, 1] = total[HROWS:]
            zsend[c] = ysum[c, 1 - half].astype(BF16)
            grad_copy(c).start()

    def pass_on(blocks):
        for q in blocks:
            z_arrival(q).wait_recv()
            for step in (1, 2, 4):
                if step > q:
                    z_block(q, step).start()

    def piece_on(b, e, frm):
        first, count = HB[b]
        block = hg.at[pl.ds(first, count), frm]
        i = b * 3 + e - 1
        return copy(block, block, hy_s.at[i], hy_r.at[i], at_y(y + e))

    def pieces_on(b):
        first, count = HB[b]
        for f in range(first, first + count):
            if f != 4:
                piece_to(f).wait_recv()
        for e in (1, 2, 3):
            piece_on(b, e, y).start()

    pass_on((1, 2, 4))
    forward(1)
    load_w.wait()
    x_arrivals(0)
    part_chunks(0, NCH)
    pass_on((3,))
    forward(2)
    pass_on((5,))
    forward(3)
    pass_on((6, 7))
    forward(4)
    pieces_on(0)
    pieces_on(1)
    pieces_on(2)
    sum_chunks(0, NCH)

    def mixed_copy(e):
        return copy(msend.at[(row + e) % X], mrecv.at[e - 1], m_s.at[e - 1], m_r.at[e - 1], at_x(row + e))

    partial = jnp.dot(hid[...], w[...], preferred_element_type=F32)
    for r in range(X):
        msend[r] = partial[r * OWN : (r + 1) * OWN].astype(BF16)
    for e in (1, 2, 3):
        mixed_copy(e).start()

    @pl.loop(0, NCH)
    def _(c):
        at = pl.ds(pl.multiple_of(c * CH, CH), CH)
        rows = pl.ds(pl.multiple_of(col * HROWS, HROWS), HROWS)
        g = gate[rows, at].astype(F32)
        sg = jax.nn.sigmoid(g)
        gate_factor[c] = up[rows, at].astype(F32) * sg * (1.0 + g * (1.0 - sg))
        up_factor[c] = g * sg

    for b in range(len(HB)):
        for e in (1, 2, 3):
            piece_on(b, e, (y - e + Y) % Y).wait_recv()
    for b in range(1, len(XB)):
        x_arrivals(b)

    def sums(chip):
        acc[...] = jnp.zeros_like(acc)

        @pl.loop(0, NT)
        def _(g):
            product = jnp.dot(
                hg[g, pl.ds(chip * 2, 2)].reshape(SHARD, TOK),
                cg[slot_of((zl + 8 - 2 * g + ZL) % ZL)],
                preferred_element_type=F32,
            )
            acc[0] += product[:PIECE]
            acc[1] += product[PIECE:]

    def chip_copy(k):
        return copy(nsend.at[k], nrecv.at[k], n_s.at[k], n_r.at[k], next_chip[k])

    sums(1 - odd)
    nsend[0] = acc[core].astype(BF16)
    nsend[1] = acc[1 - core].astype(BF16)
    chip_copy(0).start()
    chip_copy(1).start()
    sums(odd)
    swap = copy(acc.at[1 - core], arecv, a_s, a_r, other_core)
    swap.start()

    total = msend[row].astype(F32)
    for e in (1, 2, 3):
        mixed_copy(e).wait_recv()
        total = total + mrecv[e - 1].astype(F32)
    mixed[...] = total.astype(BF16)
    store_mixed = pltpu.make_async_copy(mixed, mixed_out, out_s.at[0])
    store_mixed.start()

    swap.wait_recv()
    total = acc[core] + arecv[...]
    for k in (0, 1):
        chip_copy(k).wait_recv()
        total = total + nrecv[k].astype(F32)
    weight_grad[...] = total * (1.0 / (2 * ZL))
    store_weight = pltpu.make_async_copy(weight_grad, weight_grad_out, out_s.at[1])
    store_weight.start()

    @pl.loop(0, NCH)
    def _(c):
        at = pl.ds(pl.multiple_of(c * CH, CH), CH)
        grad_copy(c).wait_recv()
        hidden_grad = ysum[c, half] + zrecv[c].astype(F32)
        gate_grad[:, at] = (hidden_grad * gate_factor[c]).astype(BF16)
        up_grad[:, at] = (hidden_grad * up_factor[c]).astype(BF16)

    store_gate = pltpu.make_async_copy(gate_grad, gate_grad_out, out_s.at[2])
    store_up = pltpu.make_async_copy(up_grad, up_grad_out, out_s.at[3])
    store_gate.start()
    store_up.start()

    for step in (1, 2, 4):
        for q in range(step):
            z_block(q, step).wait_send()
    for b in range(len(XB)):
        for e in (1, 2, 3):
            x_batch(b, e).wait_send()

    @pl.loop(0, NT)
    def _(g):
        @pl.when(g != 4)
        def _():
            piece_to(g).wait_send()

    @pl.loop(0, NCH)
    def _(c):
        for e in (1, 2, 3):
            part_copy(c, e).wait_send()
        grad_copy(c).wait_send()

    for e in (1, 2, 3):
        for b in range(len(HB)):
            piece_on(b, e, y).wait_send()
        mixed_copy(e).wait_send()
    swap.wait_send()
    for k in (0, 1):
        chip_copy(k).wait_send()
    for store in (store_mixed, store_weight, store_gate, store_up):
        store.wait()


def body(gate_pre, up_pre, down_weight, cotangent):
    hbm = pl.BlockSpec(memory_space=pltpu.HBM)
    dma = pltpu.SemaphoreType.DMA
    pair = lambda n: [dma((n,)), dma((n,))]
    return pl.pallas_call(
        kernel,
        name="mlp",
        out_shape=(
            jax.ShapeDtypeStruct((OWN, COLS), BF16),
            jax.ShapeDtypeStruct((HROWS, UNITS), BF16),
            jax.ShapeDtypeStruct((HROWS, UNITS), BF16),
            jax.ShapeDtypeStruct((SHARD // 2, COLS), F32),
        ),
        in_specs=[hbm] * 4,
        out_specs=(hbm,) * 4,
        scratch_shapes=[
            pltpu.VMEM((OWN, COLS), BF16),
            pltpu.VMEM((HROWS, UNITS), BF16),
            pltpu.VMEM((HROWS, UNITS), BF16),
            pltpu.VMEM((SHARD // 2, COLS), F32),
            pltpu.VMEM((NCH, HROWS, CH), F32),
            pltpu.VMEM((NCH, HROWS, CH), F32),
            pltpu.VMEM((TOK, UNITS), BF16),
            pltpu.VMEM((TOK, UNITS), BF16),
            pltpu.VMEM((UNITS, COLS), BF16),
            pltpu.VMEM((TOK, UNITS), BF16),
            pltpu.VMEM((UNITS, TOK), BF16),
            pltpu.VMEM((NT, TOK, COLS), BF16),
            pltpu.VMEM((NT, Y, PIECE, TOK), BF16),
            pltpu.VMEM((NCH, TOK, CH), BF16),
            pltpu.VMEM((NCH, 3, 2 * HROWS, CH), BF16),
            pltpu.VMEM((NCH, 2, HROWS, CH), F32),
            pltpu.VMEM((NCH, HROWS, CH), BF16),
            pltpu.VMEM((NCH, HROWS, CH), BF16),
            pltpu.VMEM((X, OWN, COLS), BF16),
            pltpu.VMEM((3, OWN, COLS), BF16),
            pltpu.VMEM((2, SHARD // 2, COLS), F32),
            pltpu.VMEM((SHARD // 2, COLS), F32),
            pltpu.VMEM((2, SHARD // 2, COLS), BF16),
            pltpu.VMEM((2, SHARD // 2, COLS), BF16),
            dma((4,)), dma((4,)), *pair(NT), *pair(3 * len(XB)), *pair(NT), *pair(3 * len(HB)), *pair(3 * NCH), *pair(NCH), *pair(3),
            dma, dma, *pair(2),
        ],
        compiler_params=pltpu.CompilerParams(
            collective_id=0, has_side_effects=True, vmem_limit_bytes=60 << 20
        ),
    )(gate_pre, up_pre, down_weight, cotangent)


def solution(mesh):
    placed = (P("dp", "row"), P("dp", "row"), P("row", "col"), P(("dp", "row"), "col"))
    return jax.shard_map(
        body,
        mesh=mesh,
        in_specs=placed,
        out_specs=(
            P(("dp", "row"), "col"),
            P(("dp", "col"), "row"),
            P(("dp", "col"), "row"),
            P(("row", "dp"), "col"),
        ),
        check_vma=False,
    )
```

```python
import functools

import jax
import jax.numpy as jnp
from jax import lax
from jax.experimental import pallas as pl
from jax.experimental.pallas import tpu as pltpu
from jax.sharding import PartitionSpec as P

F32, BF16 = jnp.float32, jnp.bfloat16
ZL, X, Y = 16, 4, 4
TOK, UNITS, COLS = 128, 3584, 512
OWN = TOK // X
HROWS = TOK // (2 * Y)
CH, NCH = 512, UNITS // 512
SHARD = UNITS // ZL
PIECE = 2 * SHARD // Y
NT = ZL // 2
XB = ((0, 1), (1, 1), (2, 2), (4, 2), (6, 2))
HB = ((2, 4), (0, 2), (6, 2))


def flip(value, mask):
    out = 0
    for bit in (1, 2, 4, 8):
        have = (value // bit) % 2
        out = out + bit * (1 - have if mask & bit else have)
    return out


def kernel(
    gate_in, up_in, w_in, cot_in, mixed, gate_grad, up_grad, weight_grad,
    gate_factor, up_factor, gate, up, w, hid, hid_t, cg, hg, part, yrecv, ysum, zsend, zrecv, msend, mrecv, acc, arecv, nsend, nrecv,
    in_s, cz_s, cz_r, cx_s, cx_r, h_s, h_r, hy_s, hy_r, p_s, p_r, g_s, g_r, m_s, m_r, a_s, a_r, n_s, n_r,
):
    dp, row, col = lax.axis_index("dp"), lax.axis_index("row"), lax.axis_index("col")
    zl, core = dp // 2, dp % 2
    y, half = col // 2, col % 2
    z = half * ZL + zl

    def slot_of(j):
        return ((j // 2) % 2) * 4 + ((j // 4) % 2) * 2 + j // 8

    slot = slot_of(zl)
    mine = pl.ds(pl.multiple_of(row * OWN, OWN), OWN)
    load_cot = pltpu.make_async_copy(cot_in, cg.at[slot, mine], in_s.at[0])
    load_w = pltpu.make_async_copy(w_in, w, in_s.at[1])
    load_gate = pltpu.make_async_copy(gate_in, gate, in_s.at[2])
    load_up = pltpu.make_async_copy(up_in, up, in_s.at[3])
    for load in (load_cot, load_gate, load_up, load_w):
        load.start()

    def at_z(to):
        to = (to + 4 * ZL) % (2 * ZL)
        return {"dp": (to % ZL) * 2 + core, "row": row, "col": y * 2 + to // ZL}

    def at_y(to):
        return {"dp": dp, "row": row, "col": ((to + Y) % Y) * 2 + half}

    def at_x(to):
        return {"dp": dp, "row": (to + X) % X, "col": col}

    other_core = {"dp": zl * 2 + 1 - core, "row": row, "col": col}
    odd = zl % 2
    next_zl = flip(zl, 1)
    next_chip = ({"dp": next_zl * 2 + core, "row": row, "col": col}, {"dp": next_zl * 2 + 1 - core, "row": row, "col": col})

    def copy(src, dst, send, recv, to):
        return pltpu.make_async_remote_copy(
            src_ref=src, dst_ref=dst, send_sem=send, recv_sem=recv,
            device_id=to, device_id_type=pl.DeviceIdType.MESH,
        )

    barrier = pltpu.get_barrier_semaphore()

    def greet(to):
        pl.semaphore_signal(barrier, inc=1, device_id=to, device_id_type=pl.DeviceIdType.MESH)

    for e in (1, 2, 3):
        greet(at_x(row + e))
        greet(at_y(y + e))
    greet(other_core)
    greet(next_chip[0])
    greet(next_chip[1])

    @pl.loop(1, 5)
    def _(i):
        greet(at_z(z + 2 * i))
        greet(at_z(z - 2 * i))

    load_gate.wait()
    load_up.wait()

    @pl.loop(0, NCH)
    def _(c):
        at = pl.ds(pl.multiple_of(c * CH, CH), CH)
        g = gate[:, at].astype(F32)
        h = (g * jax.nn.sigmoid(g)) * up[:, at].astype(F32)
        hid[:, at] = h.astype(BF16)
        hid_t[at, :] = h.T.astype(BF16)

    def piece(i):
        return pl.ds(pl.multiple_of((i // 2) * 2 * SHARD + y * PIECE, 16), PIECE)

    def piece_to(g):
        rows = piece((zl + 2 * g + 8) % ZL)
        far = (1 - jnp.minimum(g, 1)) * ((zl // 2) % 2) * ZL
        return copy(hid_t.at[rows], hg.at[g, y], h_s.at[g], h_r.at[g], at_z(z + 2 * g - 8 + far))

    def send_pieces():
        @pl.loop(0, NT)
        def _(g):
            @pl.when(g != 4)
            def _():
                piece_to(g).start()

    hg[4, y] = hid_t[piece(zl), :]
    pl.semaphore_wait(barrier, 17)

    def z_block(q, step):
        block = cg.at[flip(slot, q), mine]
        to = at_z(half * ZL + flip(zl, {1: 8, 2: 4, 4: 2}[step]))
        return copy(block, block, cz_s.at[q + step], cz_r.at[q + step], to)

    def z_arrival(q):
        block = cg.at[flip(slot, q), mine]
        return copy(block, block, cz_s.at[q], cz_r.at[q], at_z(z + 1))

    def x_batch(b, e, frm=None):
        first, count = XB[b]
        start = (flip(slot, first) // count) * count
        rows = mine if frm is None else pl.ds(pl.multiple_of(((frm + X) % X) * OWN, OWN), OWN)
        block = cg.at[pl.ds(start, count), rows]
        i = b * 3 + e - 1
        return copy(block, block, cx_s.at[i], cx_r.at[i], at_x(row + e))

    def forward(b):
        for e in (1, 2, 3):
            x_batch(b, e).start()

    def x_arrivals(b):
        for e in (1, 2, 3):
            x_batch(b, e, row - e).wait_recv()

    load_cot.wait()
    forward(0)
    for step in (1, 2, 4):
        z_block(0, step).start()

    send_pieces()

    def part_copy(c, e):
        rows = pl.ds(pl.multiple_of(((y + e) % Y) * 2 * HROWS, 2 * HROWS), 2 * HROWS)
        i = c * 3 + e - 1
        return copy(part.at[c, rows], yrecv.at[c, e - 1], p_s.at[i], p_r.at[i], at_y(y + e))

    def part_chunks(first, last):
        @pl.loop(first, last)
        def _(c):
            at = pl.ds(pl.multiple_of(c * CH, CH), CH)
            part[c] = lax.dot_general(
                cg[slot], w[at, :], (((1,), (1,)), ((), ())), preferred_element_type=F32
            ).astype(BF16)
            for e in (1, 2, 3):
                part_copy(c, e).start()

    def grad_copy(c):
        return copy(zsend.at[c], zrecv.at[c], g_s.at[c], g_r.at[c], at_z(z + ZL))

    def sum_chunks(first, last):
        @pl.loop(first, last)
        def _(c):
            own = pl.ds(pl.multiple_of(y * 2 * HROWS, 2 * HROWS), 2 * HROWS)
            total = part[c, own].astype(F32)
            for e in (1, 2, 3):
                part_copy(c, e).wait_recv()
                total = total + yrecv[c, e - 1].astype(F32)
            ysum[c, 0] = total[:HROWS]
            ysum[c, 1] = total[HROWS:]
            zsend[c] = ysum[c, 1 - half].astype(BF16)
            grad_copy(c).start()

    def pass_on(blocks):
        for q in blocks:
            z_arrival(q).wait_recv()
            for step in (1, 2, 4):
                if step > q:
                    z_block(q, step).start()

    def piece_on(b, e, frm):
        first, count = HB[b]
        block = hg.at[pl.ds(first, count), frm]
        i = b * 3 + e - 1
        return copy(block, block, hy_s.at[i], hy_r.at[i], at_y(y + e))

    def pieces_on(b):
        first, count = HB[b]
        for f in range(first, first + count):
            if f != 4:
                piece_to(f).wait_recv()
        for e in (1, 2, 3):
            piece_on(b, e, y).start()

    pass_on((1, 2, 4))
    forward(1)
    load_w.wait()
    x_arrivals(0)
    part_chunks(0, NCH)
    pass_on((3,))
    forward(2)
    pass_on((5,))
    forward(3)
    pass_on((6, 7))
    forward(4)
    pieces_on(0)
    pieces_on(1)
    pieces_on(2)
    sum_chunks(0, NCH)

    def mixed_copy(e):
        return copy(msend.at[(row + e) % X], mrecv.at[e - 1], m_s.at[e - 1], m_r.at[e - 1], at_x(row + e))

    partial = jnp.dot(hid[...], w[...], preferred_element_type=F32)
    for r in range(X):
        msend[r] = partial[r * OWN : (r + 1) * OWN].astype(BF16)
    for e in (1, 2, 3):
        mixed_copy(e).start()

    @pl.loop(0, NCH)
    def _(c):
        at = pl.ds(pl.multiple_of(c * CH, CH), CH)
        rows = pl.ds(pl.multiple_of(col * HROWS, HROWS), HROWS)
        g = gate[rows, at].astype(F32)
        sg = jax.nn.sigmoid(g)
        gate_factor[c] = up[rows, at].astype(F32) * sg * (1.0 + g * (1.0 - sg))
        up_factor[c] = g * sg

    for b in range(len(HB)):
        for e in (1, 2, 3):
            piece_on(b, e, (y - e + Y) % Y).wait_recv()
    for b in range(1, len(XB)):
        x_arrivals(b)

    def sums(chip):
        acc[...] = jnp.zeros_like(acc)

        @pl.loop(0, NT)
        def _(g):
            product = jnp.dot(
                hg[g, pl.ds(chip * 2, 2)].reshape(SHARD, TOK),
                cg[slot_of((zl + 8 - 2 * g + ZL) % ZL)],
                preferred_element_type=F32,
            )
            acc[0] += product[:PIECE]
            acc[1] += product[PIECE:]

    def chip_copy(k):
        return copy(nsend.at[k], nrecv.at[k], n_s.at[k], n_r.at[k], next_chip[k])

    sums(1 - odd)
    nsend[0] = acc[core].astype(BF16)
    nsend[1] = acc[1 - core].astype(BF16)
    chip_copy(0).start()
    chip_copy(1).start()
    sums(odd)
    swap = copy(acc.at[1 - core], arecv, a_s, a_r, other_core)
    swap.start()

    total = msend[row].astype(F32)
    for e in (1, 2, 3):
        mixed_copy(e).wait_recv()
        total = total + mrecv[e - 1].astype(F32)
    mixed[...] = total.astype(BF16)

    swap.wait_recv()
    total = acc[core] + arecv[...]
    for k in (0, 1):
        chip_copy(k).wait_recv()
        total = total + nrecv[k].astype(F32)
    weight_grad[...] = total * (1.0 / (2 * ZL))

    @pl.loop(0, NCH)
    def _(c):
        at = pl.ds(pl.multiple_of(c * CH, CH), CH)
        grad_copy(c).wait_recv()
        hidden_grad = ysum[c, half] + zrecv[c].astype(F32)
        gate_grad[:, at] = (hidden_grad * gate_factor[c]).astype(BF16)
        up_grad[:, at] = (hidden_grad * up_factor[c]).astype(BF16)

    for step in (1, 2, 4):
        for q in range(step):
            z_block(q, step).wait_send()
    for b in range(len(XB)):
        for e in (1, 2, 3):
            x_batch(b, e).wait_send()

    @pl.loop(0, NT)
    def _(g):
        @pl.when(g != 4)
        def _():
            piece_to(g).wait_send()

    @pl.loop(0, NCH)
    def _(c):
        for e in (1, 2, 3):
            part_copy(c, e).wait_send()
        grad_copy(c).wait_send()

    for e in (1, 2, 3):
        for b in range(len(HB)):
            piece_on(b, e, y).wait_send()
        mixed_copy(e).wait_send()
    swap.wait_send()
    for k in (0, 1):
        chip_copy(k).wait_send()


def hand_over(a, b, c, d, a_out, b_out, c_out, d_out, sems):
    copies = [
        pltpu.make_async_copy(src, dst, sems.at[i])
        for i, (src, dst) in enumerate(((a, a_out), (b, b_out), (c, c_out), (d, d_out)))
    ]
    for c in copies:
        c.start()
    for c in copies:
        c.wait()


def body(gate_pre, up_pre, down_weight, cotangent):
    hbm = pl.BlockSpec(memory_space=pltpu.HBM)
    vmem = pl.BlockSpec(memory_space=pltpu.VMEM)
    dma = pltpu.SemaphoreType.DMA
    pair = lambda n: [dma((n,)), dma((n,))]
    shapes = (
        jax.ShapeDtypeStruct((OWN, COLS), BF16),
        jax.ShapeDtypeStruct((HROWS, UNITS), BF16),
        jax.ShapeDtypeStruct((HROWS, UNITS), BF16),
        jax.ShapeDtypeStruct((SHARD // 2, COLS), F32),
    )
    results = pl.pallas_call(
        kernel,
        name="mlp",
        out_shape=shapes,
        in_specs=[hbm] * 4,
        out_specs=(vmem,) * 4,
        scratch_shapes=[
            pltpu.VMEM((NCH, HROWS, CH), F32),
            pltpu.VMEM((NCH, HROWS, CH), F32),
            pltpu.VMEM((TOK, UNITS), BF16),
            pltpu.VMEM((TOK, UNITS), BF16),
            pltpu.VMEM((UNITS, COLS), BF16),
            pltpu.VMEM((TOK, UNITS), BF16),
            pltpu.VMEM((UNITS, TOK), BF16),
            pltpu.VMEM((NT, TOK, COLS), BF16),
            pltpu.VMEM((NT, Y, PIECE, TOK), BF16),
            pltpu.VMEM((NCH, TOK, CH), BF16),
            pltpu.VMEM((NCH, 3, 2 * HROWS, CH), BF16),
            pltpu.VMEM((NCH, 2, HROWS, CH), F32),
            pltpu.VMEM((NCH, HROWS, CH), BF16),
            pltpu.VMEM((NCH, HROWS, CH), BF16),
            pltpu.VMEM((X, OWN, COLS), BF16),
            pltpu.VMEM((3, OWN, COLS), BF16),
            pltpu.VMEM((2, SHARD // 2, COLS), F32),
            pltpu.VMEM((SHARD // 2, COLS), F32),
            pltpu.VMEM((2, SHARD // 2, COLS), BF16),
            pltpu.VMEM((2, SHARD // 2, COLS), BF16),
            dma((4,)), *pair(NT), *pair(3 * len(XB)), *pair(NT), *pair(3 * len(HB)), *pair(3 * NCH), *pair(NCH), *pair(3),
            dma, dma, *pair(2),
        ],
        compiler_params=pltpu.CompilerParams(
            collective_id=0, has_side_effects=True, vmem_limit_bytes=60 << 20
        ),
    )(gate_pre, up_pre, down_weight, cotangent)
    return pl.pallas_call(
        hand_over,
        name="results",
        out_shape=shapes,
        in_specs=[vmem] * 4,
        out_specs=(hbm,) * 4,
        scratch_shapes=[dma((4,))],
    )(*results)


def solution(mesh):
    placed = (P("dp", "row"), P("dp", "row"), P("row", "col"), P(("dp", "row"), "col"))
    return jax.shard_map(
        body,
        mesh=mesh,
        in_specs=placed,
        out_specs=(
            P(("dp", "row"), "col"),
            P(("dp", "col"), "row"),
            P(("dp", "col"), "row"),
            P(("row", "dp"), "col"),
        ),
        check_vma=False,
    )
```
